128 devices in a mesh: tm: 2 (over core), cls: 64 (over z, x, y).
Axes of the slice: x: 4, y: 4, z: 4, core: 2. Of those that a mesh axis runs over, the one named last changes fastest.
Arguments:
- visibilities: bfloat16 [32768, 3072], P(('tm', 'cls')), may hold values from -6 to 6
- row_class: int32 [32768, 1], P(('tm', 'cls')), may hold values from 0 to 255; in each aligned block of 256 rows (0 to 255, 256 to 511, ...) at most 2 rows name the same one
- filters: bfloat16 [256, 1536, 1536], P(('tm', 'cls'))
- flags: int32 [256, 1536], P(('tm', 'cls')), may hold values 0 or 1
- taper: float32 [1536], replicated, may hold values from 0.2 to 1
- pairs: int32 [32768, 2], P(('tm', 'cls')), may hold values from 0 to 32767, as said below
Outputs:
- power: float32 [32768, 1536], P(('tm', 'cls'))
The draws below stay inside these ranges and needn't reach their ends.
Inputs may be any that keep to these rules, and one draw needn't show every extreme that they name: `row_class`: among the rows of one device at most 2 have any one class, and some class has exactly 2 of them. `pairs`: both entries of row p name rows of the same aligned block of 256 rows as p; the first column is a permutation of that block.
All inputs are finite; a program needn't handle non-finite values. No bound on the sum of `flags` on one device may be relied on, other than what follows from the above.
Results may differ from the reference program's by a relative error of at most 0.0068.
Values may be sent and summed in bfloat16 or wider, within the bound.
No kernel may reach another device: no remote copies, remote signals or barrier semaphores. Data moves between devices by JAX's collectives and lax.ppermute only.
A program may use at most 128 MiB of HBM per device.

```python
import math
import jax
import jax.numpy as jnp
import numpy as np
from jax import lax

NCH = 1536
ROW_DEV = 256
CLASSES = 256
ROWS = 32768
CAP = 2
N_TM = 2
N_CLS = 64


def draw_filters(key, part):
    key_diag = jax.random.fold_in(key, 11)
    key_off = jax.random.fold_in(key, 12)
    index = jnp.arange(NCH, dtype=jnp.int32)
    identity = (index[:, None] == index[None, :]).astype(jnp.float32)
    diagonal = 0.6 + 0.8 * jax.random.uniform(key_diag, (CLASSES, 1, NCH), jnp.float32)
    off = 0.02 * jax.random.normal(key_off, (CLASSES, NCH, NCH), jnp.float32)
    return (identity[None] * diagonal + off).astype(jnp.bfloat16)


def draw_pairs(key, part):
    key_order = jax.random.fold_in(key, 21)
    key_other = jax.random.fold_in(key, 22)
    blocks = ROWS // ROW_DEV
    scores = jax.random.randint(key_order, (blocks, ROW_DEV), 0, ROW_DEV) * ROW_DEV + jnp.arange(ROW_DEV, dtype=jnp.int32)[None, :]
    order = jnp.argsort(scores, axis=1, stable=True).astype(jnp.int32)
    base = (jnp.arange(blocks, dtype=jnp.int32) * ROW_DEV)[:, None]
    first = (order + base).reshape(ROWS)
    second = (jax.random.randint(key_other, (blocks, ROW_DEV), 0, ROW_DEV) + base).reshape(ROWS)
    return jnp.stack([first, second], axis=1).astype(jnp.int32)


def set_ends(result, rng, low, top_value):
    index_at = [jax.random.randint(jax.random.fold_in(rng, axis), (), 0, length) for axis, length in enumerate(result.shape)]
    longest = result.shape.index(max(result.shape))
    beside = index_at[:longest] + [(index_at[longest] + 1) % result.shape[longest]] + index_at[longest + 1:]
    return result.at[tuple(index_at)].set(low).at[tuple(beside)].set(top_value)


def block_scale(own_key, shape, split, low, high):
    factor_of, own = 1.0, jax.random.fold_in(own_key, 6)
    for dim, parts in split:
        heights = jnp.exp(jax.random.uniform(jax.random.fold_in(own, dim), (parts,), jnp.float32, low / len(split), high / len(split)))
        factor_of = factor_of * jnp.repeat(heights, shape[dim] // parts).reshape([-1 if axis == dim else 1 for axis in range(len(shape))])
    return factor_of


def shared_out(rng, own, number, rows, count, top, most, slope):
    order = jax.random.permutation(rng, count)
    packed, common = load_shares(count, rows * top, most, slope, True), load_shares(count, rows * top, most, slope, False)
    places = jnp.arange(count)

    def named(tallies, turn):
        used = int((tallies > 0).sum())
        fixed = max(1, used // 4)
        shifted = fixed + (places - fixed + turn * (used - fixed)) % max(1, count - fixed)
        return jnp.zeros((count,), jnp.int32).at[order[jnp.where(places < fixed, places, shifted)]].set(jnp.asarray(tallies, jnp.int32))

    tallies = jnp.where(number % 4 == 0, named(packed, number // 4), named(common, number - number // 4 - 1))
    mixed = jax.random.permutation(jax.random.fold_in(own, 3), count)
    giver, sink = mixed[0:count // 2 * 2:2], mixed[1:count // 2 * 2:2]
    slack = jnp.minimum(tallies[giver] - 1, most - tallies[sink]) // 2
    slack = jnp.where((giver == order[0]) | (sink == order[0]) | (tallies[sink] == 0), 0, jnp.maximum(slack, 0))
    shifted = jax.random.randint(jax.random.fold_in(own, 4), (count // 2,), 0, 1 << 20) % (slack + 1)
    tallies = tallies.at[giver].add(-shifted).at[sink].add(shifted)
    members = jnp.searchsorted(jnp.cumsum(tallies), jnp.arange(rows * top), side="right").astype(jnp.int32)
    table = members.reshape(top, rows).T
    table = table[jax.random.permutation(jax.random.fold_in(own, 1), rows)]
    turn = jax.random.randint(jax.random.fold_in(own, 2), (rows, 1), 0, top)
    return jnp.take_along_axis(table, (jnp.arange(top)[None, :] + turn) % top, axis=1)


def load_shares(count, total, limit, skew, full):
    weights = [(1 << 20) // math.isqrt(grade ** skew) + 1 for grade in range(1, count + 1)]
    largest = limit if full else min(limit, max(-(-total // count), total * weights[0] // sum(weights)))
    least = 1 if total - largest >= count - 1 else 0
    given, surplus = [largest] + [least] * (count - 1), total - largest - least * (count - 1)
    while surplus > 0:
        free = [i for i in range(1, count) if given[i] < largest] or [i for i in range(1, count) if given[i] < limit]
        whole, budget = sum([weights[i] for i in free]), surplus
        for i in free:
            extra = min(limit - given[i], max(1, budget * weights[i] // whole), surplus)
            given[i] = given[i] + extra
            surplus = surplus - extra
    return np.array(given)


def gaussian(key, extent, spread, limit, pieces=(), kind=jnp.bfloat16):
    entries = spread * jax.random.normal(key, extent, jnp.float32)
    if pieces:
        entries = entries * block_scale(key, extent, pieces, -0.22, 0.18)
    return jnp.clip(entries, -limit, limit).astype(kind)


def setup_inputs(seed: int = 0) -> dict:
    splits = jax.random.split(jax.random.key(seed), 7)
    visibilities = gaussian(splits[0], (ROWS, 2 * NCH), 1.0, 6.0, ((0, 128),))
    row_class_keys = jax.random.split(jax.random.fold_in(splits[1], 1), ROWS // ROW_DEV)
    row_class_turns = jax.random.permutation(jax.random.fold_in(splits[1], 3), ROWS // ROW_DEV)
    row_class = jax.vmap(lambda own, number: shared_out(jax.random.fold_in(splits[1], 2), own, number, ROW_DEV, CLASSES, 1, CAP, 2))(row_class_keys, row_class_turns).reshape((ROWS, 1))
    filters = draw_filters(jax.random.fold_in(splits[6], 71), 0)
    flags = set_ends((jax.random.randint(splits[3], (CLASSES, NCH), 0, 8) < 1).astype(jnp.int32), jax.random.fold_in(splits[3], 1), 0, 1)
    taper = jnp.clip(jnp.exp(jax.random.uniform(splits[4], (NCH,), jnp.float32, math.log(0.2), math.log(1.0))), 0.2, 1.0)
    pairs = draw_pairs(jax.random.fold_in(splits[6], 71), 0)
    return {"visibilities": visibilities, "row_class": row_class, "filters": filters, "flags": flags, "taper": taper, "pairs": pairs}


def dft_tables(width):
    index = jnp.arange(width, dtype=jnp.int32)
    phase = index[:, None] * index[None, :] % width
    angle = phase.astype(jnp.float32) * (2.0 * math.pi / width)
    scale = 1.0 / math.sqrt(width)
    return ((jnp.cos(angle) * scale).astype(jnp.bfloat16), (jnp.sin(angle) * scale).astype(jnp.bfloat16))

def transform(block, keep, matrix, taper, cosines, sines):
    width = matrix.shape[0]
    count = block.shape[0]
    stacked = jnp.concatenate([block[:, :width], block[:, width:]], axis=0) * keep[None, :]
    filtered = jnp.dot(stacked, matrix, preferred_element_type=jnp.float32)
    tapered = (filtered * taper[None, :]).astype(jnp.bfloat16)
    along_cos = jnp.dot(tapered, cosines, preferred_element_type=jnp.float32)
    along_sin = jnp.dot(tapered, sines, preferred_element_type=jnp.float32)
    real_part = along_cos[:count] + along_sin[count:]
    imag_part = along_cos[count:] - along_sin[:count]
    return jnp.concatenate([real_part, imag_part], axis=1).astype(jnp.bfloat16)

def reference(visibilities, row_class, filters, flags, taper, pairs):
    devices = N_TM * N_CLS
    labels = row_class[:, 0]
    onehot = (labels[:, None] == jnp.arange(CLASSES, dtype=jnp.int32)[None, :]).astype(jnp.int32)
    running = jnp.cumsum(onehot.reshape(devices, ROW_DEV, CLASSES), axis=1).reshape(ROWS, CLASSES)
    slot = lax.optimization_barrier(jnp.sum(onehot * (running - 1), axis=1)).astype(jnp.int32)
    owner_row = (jnp.arange(ROWS, dtype=jnp.int32) // ROW_DEV).astype(jnp.int32)
    position = owner_row * CAP + slot
    buffer = jnp.zeros((CLASSES, devices * CAP, 2 * NCH), jnp.bfloat16).at[labels, position].set(visibilities)
    cosines, sines = dft_tables(NCH)
    keep_all = (1 - flags).astype(jnp.bfloat16)

    def one_class(items):
        block, keep, matrix = items
        return transform(block, keep, matrix, taper, cosines, sines)
    results = lax.map(one_class, (buffer, keep_all, filters))
    spectra = results[labels, position].astype(jnp.float32)
    first = spectra[pairs[:, 0]]
    second = spectra[pairs[:, 1]]
    return first[:, :NCH] * second[:, :NCH] + first[:, NCH:] * second[:, NCH:]
```

```python
import math

import jax
import jax.numpy as jnp
from jax import lax
from jax.experimental import pallas as pl
from jax.experimental.pallas import tpu as pltpu
from jax.sharding import PartitionSpec as P

BF16 = jnp.bfloat16
F32 = jnp.float32
SLOTS = 2
PARTS = 2
TILE = 8
LIMIT = 48 << 20


def iota(shape, axis):
    return lax.broadcasted_iota(jnp.int32, shape, axis)


def row_of_slot(labels_row):
    count = labels_row.shape[1]
    across = jnp.broadcast_to(labels_row.astype(F32), (count, count))
    down = across.T
    earlier = iota((count, count), 0) < iota((count, count), 1)
    slot = jnp.sum(jnp.where((across == down) & earlier, 1.0, 0.0), axis=0, keepdims=True)
    slot = slot.astype(jnp.int32)
    return (labels_row >> 1) * TILE + (labels_row & 1) * (PARTS * SLOTS) + slot


def pack_kernel(labels_ref, real_ref, imag_ref, out_ref, select_ref):
    rows = out_ref.shape[0]
    count = real_ref.shape[0]

    @pl.when(pl.program_id(0) == 0)
    def _():
        place = row_of_slot(labels_ref[...])
        index = iota((rows, count), 0)
        select_ref[:, :count] = jnp.where(index == place, 1.0, 0.0).astype(BF16)
        select_ref[:, count:] = jnp.where(index == place + SLOTS, 1.0, 0.0).astype(BF16)

    stacked = jnp.concatenate([real_ref[...], imag_ref[...]], axis=0)
    out_ref[...] = jnp.dot(select_ref[...], stacked, preferred_element_type=F32).astype(BF16)


def pack(labels_row, visibilities, rows, width, step):
    count = visibilities.shape[0]
    steps = width // step
    return pl.pallas_call(
        pack_kernel,
        grid=(steps,),
        in_specs=[
            pl.BlockSpec((1, count), lambda j: (0, 0)),
            pl.BlockSpec((count, step), lambda j: (0, j)),
            pl.BlockSpec((count, step), lambda j: (0, j + steps)),
        ],
        out_specs=pl.BlockSpec((rows, step), lambda j: (0, j)),
        out_shape=jax.ShapeDtypeStruct((rows, width), BF16),
        scratch_shapes=[pltpu.VMEM((rows, PARTS * count), BF16)],
        compiler_params=pltpu.CompilerParams(vmem_limit_bytes=LIMIT),
        name="pack",
    )(labels_row, visibilities, visibilities)


def index_kernel(labels_ref, pairs_ref, fetch_ref, second_ref):
    count = labels_ref.shape[1]
    rows = fetch_ref.shape[1]
    place = row_of_slot(labels_ref[...])
    local = (pairs_ref[...] & (count - 1)).astype(F32)
    first = jnp.broadcast_to(local[0:1], (count, count))
    other = jnp.broadcast_to(local[1:2], (count, count))
    first_down = first.T.astype(jnp.int32)
    lane = iota((count, count), 1)
    source = jnp.sum(
        jnp.where(first_down == lane, place.astype(F32), 0.0), axis=1, keepdims=True
    ).astype(jnp.int32)
    index = iota((count, rows), 1)
    fetch_ref[:count, :] = jnp.where(index == source, 1.0, 0.0).astype(BF16)
    fetch_ref[count:, :] = jnp.where(index == source + SLOTS, 1.0, 0.0).astype(BF16)
    second_ref[...] = jnp.where(other.T == first, 1.0, 0.0).astype(BF16)


def indices(labels_row, pairs_rows, rows):
    count = labels_row.shape[1]
    return pl.pallas_call(
        index_kernel,
        out_shape=(
            jax.ShapeDtypeStruct((PARTS * count, rows), BF16),
            jax.ShapeDtypeStruct((count, count), BF16),
        ),
        compiler_params=pltpu.CompilerParams(vmem_limit_bytes=LIMIT),
        name="indices",
    )(labels_row, pairs_rows)


def table_kernel(coarse_cos_ref, coarse_sin_ref, fine_cos_ref, fine_sin_ref, cos_ref, sin_ref):
    fine = fine_cos_ref.shape[0]
    fine_cos, fine_sin = fine_cos_ref[...], fine_sin_ref[...]
    for i in range(cos_ref.shape[0] // fine):
        coarse_cos, coarse_sin = coarse_cos_ref[i : i + 1, :], coarse_sin_ref[i : i + 1, :]
        at = pl.ds(i * fine, fine)
        cos_ref[at, :] = (coarse_cos * fine_cos - coarse_sin * fine_sin).astype(BF16)
        sin_ref[at, :] = (coarse_sin * fine_cos + coarse_cos * fine_sin).astype(BF16)


def dft_tables(width, fine, step):
    def angles(rows, spacing):
        n = jnp.arange(rows, dtype=jnp.int32) * spacing
        phase = n[:, None] * jnp.arange(width, dtype=jnp.int32)[None, :] % width
        return phase.astype(F32) * (2.0 * math.pi / width)

    coarse, small = angles(width // fine, fine), angles(fine, 1)
    scale = 1.0 / math.sqrt(width)
    whole = lambda rows: pl.BlockSpec((rows, step), lambda j: (0, j))
    return pl.pallas_call(
        table_kernel,
        grid=(width // step,),
        in_specs=[whole(width // fine), whole(width // fine), whole(fine), whole(fine)],
        out_specs=(whole(width), whole(width)),
        out_shape=(jax.ShapeDtypeStruct((width, width), BF16),) * 2,
        compiler_params=pltpu.CompilerParams(vmem_limit_bytes=LIMIT),
        name="tables",
    )(jnp.cos(coarse) * scale, jnp.sin(coarse) * scale, jnp.cos(small), jnp.sin(small))


def filter_kernel(arrived_ref, flags_ref, taper_ref, filters_ref, out_ref, masked_ref):
    rows, width = arrived_ref.shape
    step = out_ref.shape[1]
    half = TILE // 2

    @pl.when(pl.program_id(0) == 0)
    def _():
        keep = (1 - flags_ref[...]).astype(F32)
        arrived = arrived_ref[...].astype(F32).reshape(rows // (2 * TILE), 2, TILE, width)
        even, odd = arrived[:, 0], arrived[:, 1]
        low = iota((1, TILE, 1), 1) < half
        first = jnp.where(low, even, pltpu.roll(odd, half, 1)) * keep[0:1][None]
        second = jnp.where(low, pltpu.roll(even, half, 1), odd) * keep[1:2][None]
        masked_ref[0] = first.reshape(rows // 2, width).astype(BF16)
        masked_ref[1] = second.reshape(rows // 2, width).astype(BF16)

    taper = taper_ref[...]
    tiled = (rows // (2 * TILE), TILE, step)
    done = [
        (jnp.dot(masked_ref[w], filters_ref[w], preferred_element_type=F32) * taper).reshape(tiled)
        for w in range(2)
    ]
    low = iota((1, TILE, 1), 1) < half
    even = jnp.where(low, done[0], pltpu.roll(done[1], half, 1))
    odd = jnp.where(low, pltpu.roll(done[0], half, 1), done[1])
    both = jnp.concatenate([even[:, None], odd[:, None]], axis=1)
    out_ref[...] = both.reshape(rows, step).astype(BF16)


def filter_rows(arrived, flags, taper_row, filters, step):
    rows, width = arrived.shape
    return pl.pallas_call(
        filter_kernel,
        grid=(width // step,),
        in_specs=[
            pl.BlockSpec((rows, width), lambda j: (0, 0), pipeline_mode=pl.Buffered(1)),
            pl.BlockSpec((2, width), lambda j: (0, 0)),
            pl.BlockSpec((1, step), lambda j: (0, j)),
            pl.BlockSpec((2, width, step), lambda j: (0, 0, j)),
        ],
        out_specs=pl.BlockSpec((rows, step), lambda j: (0, j)),
        out_shape=jax.ShapeDtypeStruct((rows, width), BF16),
        scratch_shapes=[pltpu.VMEM((2, rows // 2, width), BF16)],
        compiler_params=pltpu.CompilerParams(vmem_limit_bytes=LIMIT),
        name="filter",
    )(arrived, flags, taper_row, filters)


def power_kernel(returned_ref, fetch_ref, second_ref, cos_ref, sin_ref, out_ref, tapered_ref):
    count = second_ref.shape[0]

    @pl.when(pl.program_id(0) == 0)
    def _():
        tapered_ref[...] = jnp.dot(
            fetch_ref[...], returned_ref[...], preferred_element_type=F32
        ).astype(BF16)

    tapered = tapered_ref[...]
    along_cos = jnp.dot(tapered, cos_ref[...], preferred_element_type=F32)
    along_sin = jnp.dot(tapered, sin_ref[...], preferred_element_type=F32)
    real = (along_cos[:count] + along_sin[count:]).astype(BF16)
    imag = (along_cos[count:] - along_sin[:count]).astype(BF16)
    second = second_ref[...]
    other_real = jnp.dot(second, real, preferred_element_type=F32)
    other_imag = jnp.dot(second, imag, preferred_element_type=F32)
    out_ref[...] = real.astype(F32) * other_real + imag.astype(F32) * other_imag


def cross_power(returned, fetch, second, cosines, sines, step):
    rows, width = returned.shape
    count = second.shape[0]
    once = lambda shape: pl.BlockSpec(shape, lambda j: (0, 0), pipeline_mode=pl.Buffered(1))
    column = lambda height: pl.BlockSpec((height, step), lambda j: (0, j))
    return pl.pallas_call(
        power_kernel,
        grid=(width // step,),
        in_specs=[
            once((rows, width)),
            once(fetch.shape),
            once(second.shape),
            column(width),
            column(width),
        ],
        out_specs=column(count),
        out_shape=jax.ShapeDtypeStruct((count, width), F32),
        scratch_shapes=[pltpu.VMEM((PARTS * count, width), BF16)],
        compiler_params=pltpu.CompilerParams(vmem_limit_bytes=LIMIT),
        name="power",
    )(returned, fetch, second, cosines, sines)


def exchange(packed, peers):
    rows, width = packed.shape
    moved = lax.all_to_all(
        packed.reshape(peers, rows // peers, width),
        ("tm", "cls"),
        split_axis=0,
        concat_axis=0,
        tiled=True,
    )
    return moved.reshape(rows, width)


def local(visibilities, row_class, filters, flags, taper, pairs):
    count = visibilities.shape[0]
    classes, width = filters.shape[0], filters.shape[1]
    peers = lax.axis_size(("tm", "cls"))
    rows = peers * TILE
    assert classes == 2 and count & (count - 1) == 0
    labels_row = row_class.reshape(1, count)
    packed = pack(labels_row, visibilities, rows, width, 512)
    arrived = exchange(packed, peers)
    fetch, second = indices(labels_row, pairs.T, rows)
    cosines, sines = dft_tables(width, 32, 256)
    tapered = filter_rows(arrived, flags, taper.reshape(1, width), filters, 256)
    returned = exchange(tapered, peers)
    return cross_power(returned, fetch, second, cosines, sines, 256)


def solution(mesh):
    across = ("tm", "cls")
    placed = (
        P(across, None),
        P(across, None),
        P(across, None, None),
        P(across, None),
        P(),
        P(across, None),
    )
    return jax.shard_map(
        local, mesh=mesh, in_specs=placed, out_specs=P(across, None), check_vma=False
    )
```

```python
import math

import jax
import jax.numpy as jnp
from jax import lax
from jax.experimental import pallas as pl
from jax.experimental.pallas import tpu as pltpu
from jax.sharding import PartitionSpec as P

BF16 = jnp.bfloat16
F32 = jnp.float32
SLOTS = 2
PARTS = 2
TILE = 8


def iota(shape, axis):
    return lax.broadcasted_iota(jnp.int32, shape, axis)


def row_of_slot(labels_row):
    count = labels_row.shape[1]
    across = jnp.broadcast_to(labels_row.astype(F32), (count, count))
    down = across.T
    earlier = iota((count, count), 0) < iota((count, count), 1)
    slot = jnp.sum(jnp.where((across == down) & earlier, 1.0, 0.0), axis=0, keepdims=True)
    slot = slot.astype(jnp.int32)
    return (labels_row >> 1) * TILE + (labels_row & 1) * (PARTS * SLOTS) + slot


def pack_kernel(labels_ref, rows_hbm, out_hbm, rows_ref, select_ref, out_ref, in_sems, out_sems):
    rows, width = out_ref.shape
    count = rows_ref.shape[0] // PARTS
    steps = out_sems.shape[0]
    step = width // steps
    columns = [pl.ds(j * step, step) for j in range(steps)]
    loads = [
        [
            pltpu.make_async_copy(
                rows_hbm.at[:, pl.ds(part * width + j * step, step)],
                rows_ref.at[pl.ds(part * count, count), at],
                in_sems.at[part, j],
            )
            for part in range(PARTS)
        ]
        for j, at in enumerate(columns)
    ]
    stores = [
        pltpu.make_async_copy(out_ref.at[:, at], out_hbm.at[:, at], out_sems.at[j])
        for j, at in enumerate(columns)
    ]
    for pair in loads:
        for load in pair:
            load.start()
    place = row_of_slot(labels_ref[...])
    index = iota((rows, count), 0)
    select_ref[:, :count] = jnp.where(index == place, 1.0, 0.0).astype(BF16)
    select_ref[:, count:] = jnp.where(index == place + SLOTS, 1.0, 0.0).astype(BF16)
    for j, at in enumerate(columns):
        for load in loads[j]:
            load.wait()
        stacked = rows_ref[:, at]
        out_ref[:, at] = jnp.dot(
            select_ref[...], stacked, preferred_element_type=F32
        ).astype(BF16)
        stores[j].start()
    for store in stores:
        store.wait()


def pack(labels_row, visibilities, rows, width, step):
    count = visibilities.shape[0]
    steps = width // step
    anywhere = pl.BlockSpec(memory_space=pl.ANY)
    return pl.pallas_call(
        pack_kernel,
        in_specs=[pl.BlockSpec(memory_space=pltpu.VMEM), anywhere],
        out_specs=anywhere,
        out_shape=pltpu.HBM((rows, width), BF16),
        scratch_shapes=[
            pltpu.VMEM((PARTS * count, width), BF16),
            pltpu.VMEM((rows, PARTS * count), BF16),
            pltpu.VMEM((rows, width), BF16),
            pltpu.SemaphoreType.DMA((PARTS, steps)),
            pltpu.SemaphoreType.DMA((steps,)),
        ],
        compiler_params=pltpu.CompilerParams(vmem_limit_bytes=24 << 20),
        name="pack",
    )(labels_row, visibilities)


def index_kernel(labels_ref, pairs_ref, source_ref, second_ref):
    count = labels_ref.shape[1]
    place = row_of_slot(labels_ref[...])
    local = (pairs_ref[...] & (count - 1)).astype(F32)
    first = jnp.broadcast_to(local[0:1], (count, count))
    other = jnp.broadcast_to(local[1:2], (count, count))
    first_down = first.T.astype(jnp.int32)
    lane = iota((count, count), 1)
    source = jnp.sum(
        jnp.where(first_down == lane, place.astype(F32), 0.0), axis=1, keepdims=True
    ).astype(jnp.int32)
    source_ref[...] = source
    second_ref[...] = jnp.where(other.T == first, 1.0, 0.0).astype(BF16)


def indices(labels_row, pairs_rows):
    count = labels_row.shape[1]
    return pl.pallas_call(
        index_kernel,
        out_shape=(
            jax.ShapeDtypeStruct((count, 1), jnp.int32),
            jax.ShapeDtypeStruct((count, count), BF16),
        ),
        compiler_params=pltpu.CompilerParams(vmem_limit_bytes=24 << 20),
        name="indices",
    )(labels_row, pairs_rows)


def table_kernel(coarse_cos_ref, coarse_sin_ref, fine_cos_ref, fine_sin_ref, taper_ref, out_ref):
    fine, half = fine_cos_ref.shape
    scale = 1.0 / math.sqrt(PARTS * half)
    fine_cos, fine_sin = fine_cos_ref[...], fine_sin_ref[...]
    start = iota((fine, half), 1) == 0
    turn = jnp.where(iota((fine, half), 0) & 1 == 0, scale, -scale)
    for i in range(out_ref.shape[0] // fine):
        coarse_cos, coarse_sin = coarse_cos_ref[i : i + 1, :], coarse_sin_ref[i : i + 1, :]
        at = pl.ds(i * fine, fine)
        taper = taper_ref[at, :]
        cosines = (coarse_cos * fine_cos - coarse_sin * fine_sin).astype(BF16).astype(F32)
        sines = coarse_sin * fine_cos + coarse_cos * fine_sin
        sines = jnp.where(start, turn, sines).astype(BF16).astype(F32)
        out_ref[at, :half] = (cosines * taper).astype(BF16)
        out_ref[at, half:] = (sines * taper).astype(BF16)


def tapered_tables(width, taper_column, fine):
    half = width // 2

    def angles(rows, spacing):
        n = jnp.arange(rows, dtype=jnp.int32) * spacing
        phase = n[:, None] * jnp.arange(half, dtype=jnp.int32)[None, :] % width
        return phase.astype(F32) * (2.0 * math.pi / width)

    coarse, small = angles(width // fine, fine), angles(fine, 1)
    scale = 1.0 / math.sqrt(width)
    return pl.pallas_call(
        table_kernel,
        out_shape=jax.ShapeDtypeStruct((width, width), BF16),
        compiler_params=pltpu.CompilerParams(vmem_limit_bytes=24 << 20),
        name="tables",
    )(jnp.cos(coarse) * scale, jnp.sin(coarse) * scale, jnp.cos(small), jnp.sin(small), taper_column)


def combine_kernel(filters_ref, keep_ref, table_ref, out_ref):
    which = pl.program_id(0)
    keep = jnp.where(which == 0, keep_ref[:, 0:1], keep_ref[:, 1:2])
    product = jnp.dot(filters_ref[0], table_ref[...], preferred_element_type=F32)
    out_ref[0] = (product * keep).astype(BF16)


def combine(filters, keep_columns, table, step):
    classes, width, _ = filters.shape
    block = pl.BlockSpec((1, step, width), lambda w, i: (w, i, 0))
    return pl.pallas_call(
        combine_kernel,
        grid=(classes, width // step),
        in_specs=[
            block,
            pl.BlockSpec((step, classes), lambda w, i: (i, 0)),
            pl.BlockSpec((width, width), lambda w, i: (0, 0), pipeline_mode=pl.Buffered(1)),
        ],
        out_specs=block,
        out_shape=pltpu.HBM((classes, width, width), BF16),
        compiler_params=pltpu.CompilerParams(vmem_limit_bytes=24 << 20),
        name="combine",
    )(filters, keep_columns, table)


def filter_kernel(arrived_ref, matrix_hbm, out_hbm, split_ref, matrix_ref, out_ref, in_sems, out_sems):
    rows, width = arrived_ref.shape
    steps = in_sems.shape[0]
    step = width // steps
    half = TILE // 2
    pairs = rows // (2 * TILE)
    columns = [pl.ds(j * step, step) for j in range(steps)]
    loads = [
        pltpu.make_async_copy(matrix_hbm.at[:, :, at], matrix_ref.at[:, :, at], in_sems.at[j])
        for j, at in enumerate(columns)
    ]
    stores = [
        pltpu.make_async_copy(out_ref.at[:, at], out_hbm.at[:, at], out_sems.at[j])
        for j, at in enumerate(columns)
    ]
    for load in loads:
        load.start()
    low = iota((1, TILE, 1), 1) < half
    arrived = arrived_ref[...].astype(F32).reshape(pairs, 2, TILE, width)
    even, odd = arrived[:, 0], arrived[:, 1]
    first = jnp.where(low, even, pltpu.roll(odd, half, 1))
    second = jnp.where(low, pltpu.roll(even, half, 1), odd)
    split_ref[0] = first.reshape(rows // 2, width).astype(BF16)
    split_ref[1] = second.reshape(rows // 2, width).astype(BF16)
    for j, at in enumerate(columns):
        loads[j].wait()
        done = [
            jnp.dot(split_ref[w], matrix_ref[w, :, at], preferred_element_type=F32)
            .reshape(pairs, TILE, step)
            for w in range(2)
        ]
        even = jnp.where(low, done[0], pltpu.roll(done[1], half, 1))
        odd = jnp.where(low, pltpu.roll(done[0], half, 1), done[1])
        both = jnp.concatenate([even[:, None], odd[:, None]], axis=1)
        out_ref[:, at] = both.reshape(rows, step).astype(BF16)
        stores[j].start()
    for store in stores:
        store.wait()


def filter_rows(arrived, matrices, step):
    rows, width = arrived.shape
    anywhere = pl.BlockSpec(memory_space=pl.ANY)
    return pl.pallas_call(
        filter_kernel,
        in_specs=[pl.BlockSpec(memory_space=pltpu.VMEM), anywhere],
        out_specs=anywhere,
        out_shape=pltpu.HBM((rows, width), BF16),
        scratch_shapes=[
            pltpu.VMEM((2, rows // 2, width), BF16),
            pltpu.VMEM((2, width, width), BF16),
            pltpu.VMEM((rows, width), BF16),
            pltpu.SemaphoreType.DMA((width // step,)),
            pltpu.SemaphoreType.DMA((width // step,)),
        ],
        compiler_params=pltpu.CompilerParams(vmem_limit_bytes=40 << 20),
        name="filter",
    )(arrived, matrices)


def power_kernel(returned_ref, source_ref, second_ref, out_ref):
    count = second_ref.shape[0]
    rows, width = returned_ref.shape
    half, lanes, step = width // 2, 128, 256
    second = second_ref[...]
    index = iota((count, rows), 1)
    fetch = jnp.concatenate(
        [
            jnp.where(index == source_ref[...] + part * SLOTS, 1.0, 0.0).astype(BF16)
            for part in range(PARTS)
        ],
        axis=0,
    )
    mirror = (lanes - iota((count, lanes), 1)) & (lanes - 1)
    start = iota((count, step), 1) == 0
    mirrored = []
    for j in range(half // step):
        at = pl.ds(j * step, step)
        cos_sum = jnp.dot(fetch, returned_ref[:, at], preferred_element_type=F32)
        sin_sum = jnp.dot(
            fetch, returned_ref[:, pl.ds(half + j * step, step)], preferred_element_type=F32
        )
        cos_real, cos_imag = cos_sum[:count], cos_sum[count:]
        sin_real, sin_imag = sin_sum[:count], sin_sum[count:]
        far_real, far_imag = cos_real, cos_imag
        if j == 0:
            far_real = jnp.where(start, sin_real, cos_real)
            far_imag = jnp.where(start, sin_imag, cos_imag)
            sin_real = jnp.where(start, 0.0, sin_real)
            sin_imag = jnp.where(start, 0.0, sin_imag)
        spectra = jnp.concatenate(
            [cos_real + sin_imag, cos_imag - sin_real, far_real - sin_imag, far_imag + sin_real],
            axis=1,
        ).astype(BF16)
        other = jnp.dot(second, spectra, preferred_element_type=F32)
        product = spectra.astype(F32) * other
        out_ref[:, at] = product[:, :step] + product[:, step : 2 * step]
        far = product[:, 2 * step : 3 * step] + product[:, 3 * step :]
        for block in range(step // lanes):
            part = far[:, block * lanes : (block + 1) * lanes]
            mirrored.append(jnp.take_along_axis(part, mirror, axis=1))
    blocks = half // lanes
    first = iota((count, lanes), 1) == 0
    for b in range(blocks):
        out_ref[:, pl.ds(half + b * lanes, lanes)] = jnp.where(
            first, mirrored[(blocks - b) % blocks], mirrored[blocks - 1 - b]
        )


def cross_power(returned, source, second):
    width = returned.shape[1]
    count = second.shape[0]
    return pl.pallas_call(
        power_kernel,
        out_shape=jax.ShapeDtypeStruct((count, width), F32),
        compiler_params=pltpu.CompilerParams(vmem_limit_bytes=24 << 20),
        name="power",
    )(returned, source, second)


def exchange(packed, peers):
    rows, width = packed.shape
    moved = lax.all_to_all(
        packed.reshape(peers, rows // peers, width),
        ("tm", "cls"),
        split_axis=0,
        concat_axis=0,
        tiled=True,
    )
    return moved.reshape(rows, width)


def local(visibilities, row_class, filters, flags, taper, pairs):
    count = visibilities.shape[0]
    classes, width = filters.shape[0], filters.shape[1]
    peers = lax.axis_size(("tm", "cls"))
    rows = peers * TILE
    assert classes == 2 and count & (count - 1) == 0
    labels_row = row_class.reshape(1, count)
    in_hbm = lambda x: pltpu.with_memory_space_constraint(x, pltpu.HBM)
    packed = pack(in_hbm(labels_row), in_hbm(visibilities), rows, width, 512)
    arrived = exchange(packed, peers)
    source, second = indices(labels_row, pairs.T)
    table = tapered_tables(width, taper.reshape(width, 1), 32)
    matrices = combine(in_hbm(filters), (1 - flags).astype(F32).T, table, 512)
    summed = filter_rows(arrived, in_hbm(matrices), 256)
    returned = exchange(summed, peers)
    return cross_power(returned, source, second)


def solution(mesh):
    across = ("tm", "cls")
    placed = (
        P(across, None),
        P(across, None),
        P(across, None, None),
        P(across, None),
        P(),
        P(across, None),
    )
    return jax.shard_map(
        local, mesh=mesh, in_specs=placed, out_specs=P(across, None), check_vma=False
    )
```

```python
import functools
import math

import jax
import jax.numpy as jnp
from jax import lax
from jax.experimental import pallas as pl
from jax.experimental.pallas import tpu as pltpu
from jax.sharding import PartitionSpec as P

BF16 = jnp.bfloat16
F32 = jnp.float32
SLOTS = 2
PARTS = 2
TILE = 8


def iota(shape, axis):
    return lax.broadcasted_iota(jnp.int32, shape, axis)


def split_width(width, shares):
    unit = width // sum(shares)
    return tuple(share * unit for share in shares)


def slot_of_row(labels_row):
    count = labels_row.shape[1]
    across = jnp.broadcast_to(labels_row.astype(F32), (count, count))
    down = across.T
    earlier = iota((count, count), 0) < iota((count, count), 1)
    place = jnp.sum(jnp.where((across == down) & earlier, 1.0, 0.0), axis=0, keepdims=True)
    return labels_row * SLOTS + place.astype(jnp.int32)


def weave(first, second):
    rows, width = first.shape
    groups = (rows // TILE, TILE, width)
    first, second = first.reshape(groups), second.reshape(groups)
    low = iota((1, TILE, 1), 1) < TILE // 2
    even = jnp.where(low, first, pltpu.roll(second, TILE // 2, 1))
    odd = jnp.where(low, pltpu.roll(first, TILE // 2, 1), second)
    return jnp.concatenate([even[:, None], odd[:, None]], axis=1).reshape(2 * rows, width)


def pieces(sizes):
    starts = [sum(sizes[:i]) for i in range(len(sizes))]
    return [pl.ds(start, size) for start, size in zip(starts, sizes)]


def pack_kernel(sizes, labels_ref, rows_hbm, out_hbm, rows_ref, select_ref, out_ref, in_sems, out_sems):
    columns = pieces(sizes)
    width = out_ref.shape[1]
    loads = [
        [
            pltpu.make_async_copy(
                rows_hbm.at[:, pl.ds(part * width + at.start, at.size)],
                rows_ref.at[part, :, at],
                in_sems.at[part, j],
            )
            for part in range(PARTS)
        ]
        for j, at in enumerate(columns)
    ]
    stores = [
        pltpu.make_async_copy(out_ref.at[:, at], out_hbm.at[:, at], out_sems.at[j])
        for j, at in enumerate(columns)
    ]
    for pair in loads:
        for load in pair:
            load.start()
    select_ref[...] = jnp.where(
        iota(select_ref.shape, 0) == slot_of_row(labels_ref[...]), 1.0, 0.0
    ).astype(BF16)
    for j, at in enumerate(columns):
        for load in loads[j]:
            load.wait()
        parts = [
            jnp.dot(select_ref[...], rows_ref[part, :, at], preferred_element_type=F32)
            for part in range(PARTS)
        ]
        out_ref[:, at] = weave(*parts).astype(BF16)
        stores[j].start()
    for store in stores:
        store.wait()


def pack(labels_row, visibilities, rows, sizes):
    count, width = visibilities.shape[0], sum(sizes)
    anywhere = pl.BlockSpec(memory_space=pl.ANY)
    return pl.pallas_call(
        functools.partial(pack_kernel, sizes),
        in_specs=[pl.BlockSpec(memory_space=pltpu.VMEM), anywhere],
        out_specs=anywhere,
        out_shape=pltpu.HBM((rows, width), BF16),
        scratch_shapes=[
            pltpu.VMEM((PARTS, count, width), BF16),
            pltpu.VMEM((rows // PARTS, count), BF16),
            pltpu.VMEM((rows, width), BF16),
            pltpu.SemaphoreType.DMA((PARTS, len(sizes))),
            pltpu.SemaphoreType.DMA((len(sizes),)),
        ],
        compiler_params=pltpu.CompilerParams(vmem_limit_bytes=24 << 20),
        name="pack",
    )(labels_row, visibilities)


def index_kernel(labels_ref, pairs_ref, source_ref, second_ref):
    count = labels_ref.shape[1]
    slots = slot_of_row(labels_ref[...])
    each = TILE // PARTS
    place = slots // each * TILE + slots % each
    local = (pairs_ref[...] & (count - 1)).astype(F32)
    first = jnp.broadcast_to(local[0:1], (count, count))
    other = jnp.broadcast_to(local[1:2], (count, count))
    first_down = first.T.astype(jnp.int32)
    lane = iota((count, count), 1)
    source = jnp.sum(
        jnp.where(first_down == lane, place.astype(F32), 0.0), axis=1, keepdims=True
    ).astype(jnp.int32)
    source_ref[...] = source
    second_ref[...] = jnp.where(other.T == first, 1.0, 0.0).astype(BF16)


def indices(labels_row, pairs_rows):
    count = labels_row.shape[1]
    return pl.pallas_call(
        index_kernel,
        out_shape=(
            jax.ShapeDtypeStruct((count, 1), jnp.int32),
            jax.ShapeDtypeStruct((count, count), BF16),
        ),
        compiler_params=pltpu.CompilerParams(vmem_limit_bytes=24 << 20),
        name="indices",
    )(labels_row, pairs_rows)


def table_kernel(coarse_cos_ref, coarse_sin_ref, fine_cos_ref, fine_sin_ref, taper_ref, out_ref):
    fine, half = fine_cos_ref.shape
    scale = 1.0 / math.sqrt(PARTS * half)
    fine_cos, fine_sin = fine_cos_ref[...], fine_sin_ref[...]
    start = iota((fine, half), 1) == 0
    turn = jnp.where(iota((fine, half), 0) & 1 == 0, scale, -scale)
    for i in range(out_ref.shape[0] // fine):
        coarse_cos, coarse_sin = coarse_cos_ref[i : i + 1, :], coarse_sin_ref[i : i + 1, :]
        at = pl.ds(i * fine, fine)
        taper = taper_ref[at, :]
        cosines = (coarse_cos * fine_cos - coarse_sin * fine_sin).astype(BF16).astype(F32)
        sines = coarse_sin * fine_cos + coarse_cos * fine_sin
        sines = jnp.where(start, turn, sines).astype(BF16).astype(F32)
        out_ref[at, :half] = (cosines * taper).astype(BF16)
        out_ref[at, half:] = (sines * taper).astype(BF16)


def tapered_tables(width, taper_column, fine):
    half = width // 2

    def angles(rows, spacing):
        n = jnp.arange(rows, dtype=jnp.int32) * spacing
        phase = n[:, None] * jnp.arange(half, dtype=jnp.int32)[None, :] % width
        return phase.astype(F32) * (2.0 * math.pi / width)

    coarse, small = angles(width // fine, fine), angles(fine, 1)
    scale = 1.0 / math.sqrt(width)
    return pl.pallas_call(
        table_kernel,
        out_shape=jax.ShapeDtypeStruct((width, width), BF16),
        compiler_params=pltpu.CompilerParams(vmem_limit_bytes=24 << 20),
        name="tables",
    )(jnp.cos(coarse) * scale, jnp.sin(coarse) * scale, jnp.cos(small), jnp.sin(small), taper_column)


def combine_kernel(filters_ref, keep_ref, table_ref, out_ref):
    which = pl.program_id(0)
    keep = jnp.where(which == 0, keep_ref[:, 0:1], keep_ref[:, 1:2])
    product = jnp.dot(filters_ref[0], table_ref[...], preferred_element_type=F32)
    out_ref[0] = (product * keep).astype(BF16)


def combine(filters, keep_columns, table, step):
    classes, width, _ = filters.shape
    block = pl.BlockSpec((1, step, width), lambda w, i: (w, i, 0))
    return pl.pallas_call(
        combine_kernel,
        grid=(classes, width // step),
        in_specs=[
            block,
            pl.BlockSpec((step, classes), lambda w, i: (i, 0)),
            pl.BlockSpec((width, width), lambda w, i: (0, 0), pipeline_mode=pl.Buffered(1)),
        ],
        out_specs=block,
        out_shape=pltpu.HBM((classes, width, width), BF16),
        compiler_params=pltpu.CompilerParams(vmem_limit_bytes=24 << 20),
        name="combine",
    )(filters, keep_columns, table)


def filter_kernel(sizes, step, arrived_ref, matrix_hbm, out_hbm, split_ref, matrix_ref, out_ref, in_sems, out_sems):
    rows, width = arrived_ref.shape
    columns = pieces(sizes)
    loads = [
        pltpu.make_async_copy(matrix_hbm.at[:, :, at], matrix_ref.at[:, :, at], in_sems.at[j])
        for j, at in enumerate(columns)
    ]
    own = iota((1, TILE, 1), 1) & SLOTS == 0
    loads[0].start()
    groups = len(loads) - 1
    count = rows // (2 * groups)
    for g in range(groups):
        arrived = arrived_ref[pl.ds(2 * g * count, 2 * count), :].astype(F32)
        arrived = arrived.reshape(count // TILE, 2, TILE, width)
        even, odd = arrived[:, 0], arrived[:, 1]
        first = jnp.where(own, even, pltpu.roll(odd, SLOTS, 1))
        second = jnp.where(own, pltpu.roll(even, TILE - SLOTS, 1), odd)
        split_ref[0, pl.ds(g * count, count), :] = first.reshape(count, width).astype(BF16)
        split_ref[1, pl.ds(g * count, count), :] = second.reshape(count, width).astype(BF16)
        loads[g + 1].start()
    stores = []
    for load, piece in zip(loads, columns):
        load.wait()
        for start in range(piece.start, piece.start + piece.size, step):
            at = pl.ds(start, step)
            done = [
                jnp.dot(split_ref[w], matrix_ref[w, :, at], preferred_element_type=F32)
                .reshape(rows // (2 * TILE), TILE, step)
                for w in range(2)
            ]
            even = jnp.where(own, done[0], pltpu.roll(done[1], SLOTS, 1))
            odd = jnp.where(own, pltpu.roll(done[0], TILE - SLOTS, 1), done[1])
            both = jnp.concatenate([even[:, None], odd[:, None]], axis=1)
            out_ref[:, at] = both.reshape(rows, step).astype(BF16)
            store = pltpu.make_async_copy(
                out_ref.at[:, at], out_hbm.at[:, at], out_sems.at[len(stores)]
            )
            store.start()
            stores.append(store)
    for store in stores:
        store.wait()


def filter_rows(arrived, matrices, sizes, step):
    rows, width = arrived.shape
    anywhere = pl.BlockSpec(memory_space=pl.ANY)
    return pl.pallas_call(
        functools.partial(filter_kernel, sizes, step),
        in_specs=[pl.BlockSpec(memory_space=pltpu.VMEM), anywhere],
        out_specs=anywhere,
        out_shape=pltpu.HBM((rows, width), BF16),
        scratch_shapes=[
            pltpu.VMEM((2, rows // 2, width), BF16),
            pltpu.VMEM((2, width, width), BF16),
            pltpu.VMEM((rows, width), BF16),
            pltpu.SemaphoreType.DMA((len(sizes),)),
            pltpu.SemaphoreType.DMA((width // step,)),
        ],
        compiler_params=pltpu.CompilerParams(vmem_limit_bytes=40 << 20),
        name="filter",
    )(arrived, matrices)


def power_kernel(returned_ref, source_ref, second_ref, out_hbm, out_ref, sems):
    count = second_ref.shape[0]
    rows, width = returned_ref.shape
    half, lanes, step = width // 2, 128, 256
    second = second_ref[...]
    index = iota((count, rows), 1)
    fetch = jnp.concatenate(
        [
            jnp.where(index == source_ref[...] + part * (TILE // PARTS), 1.0, 0.0).astype(BF16)
            for part in range(PARTS)
        ],
        axis=0,
    )
    mirror = (lanes - iota((count, lanes), 1)) & (lanes - 1)
    start = iota((count, step), 1) == 0
    edge = iota((count, lanes), 1) == 0
    blocks = half // lanes
    stores = []

    def store(at):
        copy = pltpu.make_async_copy(out_ref.at[:, at], out_hbm.at[:, at], sems.at[len(stores)])
        copy.start()
        stores.append(copy)

    def spectra(sums, j):
        cos_real, cos_imag, sin_real, sin_imag = sums
        far_real, far_imag = cos_real, cos_imag
        if j == 0:
            far_real = jnp.where(start, sin_real, cos_real)
            far_imag = jnp.where(start, sin_imag, cos_imag)
            sin_real = jnp.where(start, 0.0, sin_real)
            sin_imag = jnp.where(start, 0.0, sin_imag)
        return (
            (cos_real + sin_imag, cos_imag - sin_real),
            (far_real - sin_imag, far_imag + sin_real),
        )

    mirrored = []
    waiting = list(range(blocks))
    for j in range(half // step):
        at = pl.ds(j * step, step)
        far_at = pl.ds(half + j * step, step)
        cos_sum = jnp.dot(fetch, returned_ref[:, at], preferred_element_type=F32)
        sin_sum = jnp.dot(fetch, returned_ref[:, far_at], preferred_element_type=F32)
        sums = [cos_sum[:count], cos_sum[count:], sin_sum[:count], sin_sum[count:]]
        others = jnp.dot(
            second, jnp.concatenate(sums, axis=1).astype(BF16), preferred_element_type=F32
        )
        others = [others[:, i * step : (i + 1) * step] for i in range(2 * PARTS)]
        near, far = [
            one[0] * two[0] + one[1] * two[1]
            for one, two in zip(spectra(sums, j), spectra(others, j))
        ]
        out_ref[:, at] = near
        store(at)
        for block in range(step // lanes):
            part = far[:, block * lanes : (block + 1) * lanes]
            mirrored.append(jnp.take_along_axis(part, mirror, axis=1))
        for b in list(waiting):
            edge_from, rest_from = (blocks - b) % blocks, blocks - 1 - b
            if max(edge_from, rest_from) < len(mirrored):
                waiting.remove(b)
                there = pl.ds(half + b * lanes, lanes)
                out_ref[:, there] = jnp.where(edge, mirrored[edge_from], mirrored[rest_from])
                store(there)
    for copy in stores:
        copy.wait()


def cross_power(returned, source, second):
    width = returned.shape[1]
    count = second.shape[0]
    in_vmem = pl.BlockSpec(memory_space=pltpu.VMEM)
    return pl.pallas_call(
        power_kernel,
        in_specs=[in_vmem, in_vmem, in_vmem],
        out_specs=pl.BlockSpec(memory_space=pl.ANY),
        out_shape=pltpu.HBM((count, width), F32),
        scratch_shapes=[
            pltpu.VMEM((count, width), F32),
            pltpu.SemaphoreType.DMA((width // 256 // 2 + width // 128 // 2,)),
        ],
        compiler_params=pltpu.CompilerParams(vmem_limit_bytes=24 << 20),
        name="power",
    )(returned, source, second)


def exchange(packed, peers):
    rows, width = packed.shape
    moved = lax.all_to_all(
        packed.reshape(peers, rows // peers, width),
        ("tm", "cls"),
        split_axis=0,
        concat_axis=0,
        tiled=True,
    )
    return moved.reshape(rows, width)


def local(visibilities, row_class, filters, flags, taper, pairs):
    count = visibilities.shape[0]
    classes, width = filters.shape[0], filters.shape[1]
    peers = lax.axis_size(("tm", "cls"))
    rows = peers * TILE
    assert classes == 2 and count & (count - 1) == 0
    labels_row = row_class.reshape(1, count)
    in_hbm = lambda x: pltpu.with_memory_space_constraint(x, pltpu.HBM)
    packed = pack(in_hbm(labels_row), in_hbm(visibilities), rows, split_width(width, (1, 1, 1)))
    arrived = exchange(packed, peers)
    source, second = indices(labels_row, pairs.T)
    table = tapered_tables(width, taper.reshape(width, 1), 32)
    matrices = combine(in_hbm(filters), (1 - flags).astype(F32).T, table, 512)
    summed = filter_rows(arrived, in_hbm(matrices), split_width(width, (1, 2, 3)), 256)
    returned = exchange(summed, peers)
    return cross_power(returned, source, second)


def solution(mesh):
    across = ("tm", "cls")
    placed = (
        P(across, None),
        P(across, None),
        P(across, None, None),
        P(across, None),
        P(),
        P(across, None),
    )
    return jax.shard_map(
        local, mesh=mesh, in_specs=placed, out_specs=P(across, None), check_vma=False
    )
```

```python
import functools
import math

import jax
import jax.numpy as jnp
from jax import lax
from jax.experimental import pallas as pl
from jax.experimental.pallas import tpu as pltpu
from jax.sharding import PartitionSpec as P

BF16 = jnp.bfloat16
F32 = jnp.float32
SLOTS = 2
PARTS = 2
TILE = 8


def iota(shape, axis):
    return lax.broadcasted_iota(jnp.int32, shape, axis)


def split_width(width, shares):
    unit = width // sum(shares)
    return tuple(share * unit for share in shares)


def slot_of_row(labels_row):
    count = labels_row.shape[1]
    across = jnp.broadcast_to(labels_row.astype(F32), (count, count))
    down = across.T
    earlier = iota((count, count), 0) < iota((count, count), 1)
    place = jnp.sum(jnp.where((across == down) & earlier, 1.0, 0.0), axis=0, keepdims=True)
    return labels_row * SLOTS + place.astype(jnp.int32)


def weave(first, second):
    rows, width = first.shape
    groups = (rows // TILE, TILE, width)
    first, second = first.reshape(groups), second.reshape(groups)
    low = iota((1, TILE, 1), 1) < TILE // 2
    even = jnp.where(low, first, pltpu.roll(second, TILE // 2, 1))
    odd = jnp.where(low, pltpu.roll(first, TILE // 2, 1), second)
    return jnp.concatenate([even[:, None], odd[:, None]], axis=1).reshape(2 * rows, width)


def pieces(sizes):
    starts = [sum(sizes[:i]) for i in range(len(sizes))]
    return [pl.ds(start, size) for start, size in zip(starts, sizes)]


def pack_kernel(sizes, labels_ref, rows_hbm, out_hbm, rows_ref, select_ref, out_ref, in_sems, out_sems):
    columns = pieces(sizes)
    width = out_ref.shape[1]
    loads = [
        [
            pltpu.make_async_copy(
                rows_hbm.at[:, pl.ds(part * width + at.start, at.size)],
                rows_ref.at[part, :, at],
                in_sems.at[part, j],
            )
            for part in range(PARTS)
        ]
        for j, at in enumerate(columns)
    ]
    stores = [
        pltpu.make_async_copy(out_ref.at[:, at], out_hbm.at[:, at], out_sems.at[j])
        for j, at in enumerate(columns)
    ]
    for pair in loads:
        for load in pair:
            load.start()
    select_ref[...] = jnp.where(
        iota(select_ref.shape, 0) == slot_of_row(labels_ref[...]), 1.0, 0.0
    ).astype(BF16)
    for j, at in enumerate(columns):
        for load in loads[j]:
            load.wait()
        parts = [
            jnp.dot(select_ref[...], rows_ref[part, :, at], preferred_element_type=F32)
            for part in range(PARTS)
        ]
        out_ref[:, at] = weave(*parts).astype(BF16)
        stores[j].start()
    for store in stores:
        store.wait()


def pack(labels_row, visibilities, rows, sizes):
    count, width = visibilities.shape[0], sum(sizes)
    anywhere = pl.BlockSpec(memory_space=pl.ANY)
    return pl.pallas_call(
        functools.partial(pack_kernel, sizes),
        in_specs=[pl.BlockSpec(memory_space=pltpu.VMEM), anywhere],
        out_specs=anywhere,
        out_shape=pltpu.HBM((rows, width), BF16),
        scratch_shapes=[
            pltpu.VMEM((PARTS, count, width), BF16),
            pltpu.VMEM((rows // PARTS, count), BF16),
            pltpu.VMEM((rows, width), BF16),
            pltpu.SemaphoreType.DMA((PARTS, len(sizes))),
            pltpu.SemaphoreType.DMA((len(sizes),)),
        ],
        compiler_params=pltpu.CompilerParams(vmem_limit_bytes=24 << 20),
        name="pack",
    )(labels_row, visibilities)


def index_kernel(labels_ref, pairs_ref, source_ref, second_ref):
    count = labels_ref.shape[1]
    slots = slot_of_row(labels_ref[...])
    each = TILE // PARTS
    place = slots // each * TILE + slots % each
    local = (pairs_ref[...] & (count - 1)).astype(F32)
    first = jnp.broadcast_to(local[0:1], (count, count))
    other = jnp.broadcast_to(local[1:2], (count, count))
    first_down = first.T.astype(jnp.int32)
    lane = iota((count, count), 1)
    source = jnp.sum(
        jnp.where(first_down == lane, place.astype(F32), 0.0), axis=1, keepdims=True
    ).astype(jnp.int32)
    source_ref[...] = source
    second_ref[...] = jnp.where(other.T == first, 1.0, 0.0).astype(BF16)


def indices(labels_row, pairs_rows):
    count = labels_row.shape[1]
    return pl.pallas_call(
        index_kernel,
        out_shape=(
            jax.ShapeDtypeStruct((count, 1), jnp.int32),
            jax.ShapeDtypeStruct((count, count), BF16),
        ),
        compiler_params=pltpu.CompilerParams(vmem_limit_bytes=24 << 20),
        name="indices",
    )(labels_row, pairs_rows)


def as_column(row):
    lanes = 128
    parts = [
        jnp.broadcast_to(row[:, i : i + lanes], (lanes, lanes)).T[:, 0:1]
        for i in range(0, row.shape[1], lanes)
    ]
    return jnp.concatenate(parts, axis=0)


def table_kernel(coarse_cos_ref, coarse_sin_ref, fine_cos_ref, fine_sin_ref, taper_ref, out_ref):
    fine, half = fine_cos_ref.shape
    scale = 1.0 / math.sqrt(PARTS * half)
    fine_cos, fine_sin = fine_cos_ref[...], fine_sin_ref[...]
    start = iota((fine, half), 1) == 0
    turn = jnp.where(iota((fine, half), 0) & 1 == 0, scale, -scale)
    taper = as_column(taper_ref[...])
    for i in range(out_ref.shape[1] // fine):
        coarse_cos, coarse_sin = coarse_cos_ref[i : i + 1, :], coarse_sin_ref[i : i + 1, :]
        at = pl.ds(i * fine, fine)
        cosines = coarse_cos * fine_cos - coarse_sin * fine_sin
        sines = coarse_sin * fine_cos + coarse_cos * fine_sin
        sines = jnp.where(start, turn, sines)
        for table, columns in ((cosines, pl.ds(0, half)), (sines, pl.ds(half, half))):
            tapered = table.astype(BF16).astype(F32) * taper[i * fine : (i + 1) * fine]
            high = tapered.astype(BF16)
            out_ref[0, at, columns] = high
            out_ref[1, at, columns] = (tapered - high.astype(F32)).astype(BF16)


def tapered_tables(width, taper_row, fine):
    half = width // 2

    def angles(rows, spacing):
        n = jnp.arange(rows, dtype=jnp.int32) * spacing
        phase = n[:, None] * jnp.arange(half, dtype=jnp.int32)[None, :] % width
        return phase.astype(F32) * (2.0 * math.pi / width)

    coarse, small = angles(width // fine, fine), angles(fine, 1)
    scale = 1.0 / math.sqrt(width)
    return pl.pallas_call(
        table_kernel,
        out_shape=jax.ShapeDtypeStruct((2, width, width), BF16),
        compiler_params=pltpu.CompilerParams(vmem_limit_bytes=24 << 20),
        name="tables",
    )(jnp.cos(coarse) * scale, jnp.sin(coarse) * scale, jnp.cos(small), jnp.sin(small), taper_row)


def combine_kernel(filters_ref, flags_ref, table_ref, out_ref):
    flags = jnp.where(pl.program_id(0) == 0, flags_ref[0:1, :], flags_ref[1:2, :])
    keep = as_column((1 - flags).astype(F32))
    matrix = filters_ref[0]
    product = jnp.dot(matrix, table_ref[0], preferred_element_type=F32)
    product = product + jnp.dot(matrix, table_ref[1], preferred_element_type=F32)
    out_ref[0] = (product * keep).astype(BF16)


def combine(filters, flags, table, step):
    classes, width, _ = filters.shape
    block = pl.BlockSpec((1, step, width), lambda w, i: (w, i, 0))
    return pl.pallas_call(
        combine_kernel,
        grid=(classes, width // step),
        in_specs=[
            block,
            pl.BlockSpec((classes, step), lambda w, i: (0, i)),
            pl.BlockSpec((2, width, width), lambda w, i: (0, 0, 0), pipeline_mode=pl.Buffered(1)),
        ],
        out_specs=block,
        out_shape=pltpu.HBM((classes, width, width), BF16),
        compiler_params=pltpu.CompilerParams(vmem_limit_bytes=36 << 20),
        name="combine",
    )(filters, flags, table)


def filter_kernel(sizes, step, arrived_ref, matrix_hbm, out_hbm, split_ref, matrix_ref, out_ref, in_sems, out_sems):
    rows, width = arrived_ref.shape
    columns = pieces(sizes)
    loads = [
        pltpu.make_async_copy(matrix_hbm.at[:, :, at], matrix_ref.at[:, :, at], in_sems.at[j])
        for j, at in enumerate(columns)
    ]
    own = iota((1, TILE, 1), 1) & SLOTS == 0
    loads[0].start()
    groups = len(loads) - 1
    count = rows // (2 * groups)
    for g in range(groups):
        arrived = arrived_ref[pl.ds(2 * g * count, 2 * count), :].astype(F32)
        arrived = arrived.reshape(count // TILE, 2, TILE, width)
        even, odd = arrived[:, 0], arrived[:, 1]
        first = jnp.where(own, even, pltpu.roll(odd, SLOTS, 1))
        second = jnp.where(own, pltpu.roll(even, TILE - SLOTS, 1), odd)
        split_ref[0, pl.ds(g * count, count), :] = first.reshape(count, width).astype(BF16)
        split_ref[1, pl.ds(g * count, count), :] = second.reshape(count, width).astype(BF16)
        loads[g + 1].start()
    stores = []
    for load, piece in zip(loads, columns):
        load.wait()
        for start in range(piece.start, piece.start + piece.size, step):
            at = pl.ds(start, step)
            done = [
                jnp.dot(split_ref[w], matrix_ref[w, :, at], preferred_element_type=F32)
                .reshape(rows // (2 * TILE), TILE, step)
                for w in range(2)
            ]
            even = jnp.where(own, done[0], pltpu.roll(done[1], SLOTS, 1))
            odd = jnp.where(own, pltpu.roll(done[0], TILE - SLOTS, 1), done[1])
            both = jnp.concatenate([even[:, None], odd[:, None]], axis=1)
            out_ref[:, at] = both.reshape(rows, step).astype(BF16)
            store = pltpu.make_async_copy(
                out_ref.at[:, at], out_hbm.at[:, at], out_sems.at[len(stores)]
            )
            store.start()
            stores.append(store)
    for store in stores:
        store.wait()


def filter_rows(arrived, matrices, sizes, step):
    rows, width = arrived.shape
    anywhere = pl.BlockSpec(memory_space=pl.ANY)
    return pl.pallas_call(
        functools.partial(filter_kernel, sizes, step),
        in_specs=[pl.BlockSpec(memory_space=pltpu.VMEM), anywhere],
        out_specs=anywhere,
        out_shape=pltpu.HBM((rows, width), BF16),
        scratch_shapes=[
            pltpu.VMEM((2, rows // 2, width), BF16),
            pltpu.VMEM((2, width, width), BF16),
            pltpu.VMEM((rows, width), BF16),
            pltpu.SemaphoreType.DMA((len(sizes),)),
            pltpu.SemaphoreType.DMA((width // step,)),
        ],
        compiler_params=pltpu.CompilerParams(vmem_limit_bytes=40 << 20),
        name="filter",
    )(arrived, matrices)


def power_kernel(returned_ref, source_ref, second_ref, out_hbm, out_ref, sems):
    count = second_ref.shape[0]
    rows, width = returned_ref.shape
    half, lanes, step = width // 2, 128, 256
    second = second_ref[...]
    index = iota((count, rows), 1)
    fetch = jnp.concatenate(
        [
            jnp.where(index == source_ref[...] + part * (TILE // PARTS), 1.0, 0.0).astype(BF16)
            for part in range(PARTS)
        ],
        axis=0,
    )
    mirror = (lanes - iota((count, lanes), 1)) & (lanes - 1)
    start = iota((count, step), 1) == 0
    edge = iota((count, lanes), 1) == 0
    blocks = half // lanes
    stores = []

    def store(at):
        copy = pltpu.make_async_copy(out_ref.at[:, at], out_hbm.at[:, at], sems.at[len(stores)])
        copy.start()
        stores.append(copy)

    def spectra(sums, j):
        cos_real, cos_imag, sin_real, sin_imag = sums
        far_real, far_imag = cos_real, cos_imag
        if j == 0:
            far_real = jnp.where(start, sin_real, cos_real)
            far_imag = jnp.where(start, sin_imag, cos_imag)
            sin_real = jnp.where(start, 0.0, sin_real)
            sin_imag = jnp.where(start, 0.0, sin_imag)
        return (
            (cos_real + sin_imag, cos_imag - sin_real),
            (far_real - sin_imag, far_imag + sin_real),
        )

    mirrored = []
    waiting = list(range(blocks))
    for j in range(half // step):
        at = pl.ds(j * step, step)
        far_at = pl.ds(half + j * step, step)
        cos_sum = jnp.dot(fetch, returned_ref[:, at], preferred_element_type=F32)
        sin_sum = jnp.dot(fetch, returned_ref[:, far_at], preferred_element_type=F32)
        sums = [cos_sum[:count], cos_sum[count:], sin_sum[:count], sin_sum[count:]]
        others = jnp.dot(
            second, jnp.concatenate(sums, axis=1).astype(BF16), preferred_element_type=F32
        )
        others = [others[:, i * step : (i + 1) * step] for i in range(2 * PARTS)]
        near, far = [
            one[0] * two[0] + one[1] * two[1]
            for one, two in zip(spectra(sums, j), spectra(others, j))
        ]
        out_ref[:, at] = near
        store(at)
        for block in range(step // lanes):
            part = far[:, block * lanes : (block + 1) * lanes]
            mirrored.append(jnp.take_along_axis(part, mirror, axis=1))
        for b in list(waiting):
            edge_from, rest_from = (blocks - b) % blocks, blocks - 1 - b
            if max(edge_from, rest_from) < len(mirrored):
                waiting.remove(b)
                there = pl.ds(half + b * lanes, lanes)
                out_ref[:, there] = jnp.where(edge, mirrored[edge_from], mirrored[rest_from])
                store(there)
    for copy in stores:
        copy.wait()


def cross_power(returned, source, second):
    width = returned.shape[1]
    count = second.shape[0]
    in_vmem = pl.BlockSpec(memory_space=pltpu.VMEM)
    return pl.pallas_call(
        power_kernel,
        in_specs=[in_vmem, in_vmem, in_vmem],
        out_specs=pl.BlockSpec(memory_space=pl.ANY),
        out_shape=pltpu.HBM((count, width), F32),
        scratch_shapes=[
            pltpu.VMEM((count, width), F32),
            pltpu.SemaphoreType.DMA((width // 256 // 2 + width // 128 // 2,)),
        ],
        compiler_params=pltpu.CompilerParams(vmem_limit_bytes=24 << 20),
        name="power",
    )(returned, source, second)


def exchange(packed, peers):
    rows, width = packed.shape
    moved = lax.all_to_all(
        packed.reshape(peers, rows // peers, width),
        ("tm", "cls"),
        split_axis=0,
        concat_axis=0,
        tiled=True,
    )
    return moved.reshape(rows, width)


def local(visibilities, row_class, filters, flags, taper, pairs):
    count = visibilities.shape[0]
    classes, width = filters.shape[0], filters.shape[1]
    peers = lax.axis_size(("tm", "cls"))
    rows = peers * TILE
    assert classes == 2 and count & (count - 1) == 0
    labels_row = row_class.reshape(1, count)
    in_hbm = lambda x: pltpu.with_memory_space_constraint(x, pltpu.HBM)
    packed = pack(in_hbm(labels_row), in_hbm(visibilities), rows, split_width(width, (1, 1, 1)))
    arrived = exchange(packed, peers)
    source, second = indices(labels_row, pairs.T)
    table = tapered_tables(width, taper.reshape(1, width), 32)
    matrices = combine(in_hbm(filters), flags, table, 512)
    summed = filter_rows(arrived, in_hbm(matrices), split_width(width, (1, 2, 3)), 256)
    returned = exchange(summed, peers)
    return cross_power(returned, source, second)


def solution(mesh):
    across = ("tm", "cls")
    placed = (
        P(across, None),
        P(across, None),
        P(across, None, None),
        P(across, None),
        P(),
        P(across, None),
    )
    return jax.shard_map(
        local, mesh=mesh, in_specs=placed, out_specs=P(across, None), check_vma=False
    )
```

```python
import functools
import math

import jax
import jax.numpy as jnp
from jax import lax
from jax.experimental import pallas as pl
from jax.experimental.pallas import tpu as pltpu
from jax.sharding import PartitionSpec as P

BF16 = jnp.bfloat16
F32 = jnp.float32
SLOTS = 2
PARTS = 2
TILE = 8
PACKED = 16


def iota(shape, axis):
    return lax.broadcasted_iota(jnp.int32, shape, axis)


def split_width(width, shares):
    unit = width // sum(shares)
    return tuple(share * unit for share in shares)


def slot_of_row(labels_row):
    count = labels_row.shape[1]
    across = jnp.broadcast_to(labels_row.astype(F32), (count, count))
    down = across.T
    earlier = iota((count, count), 0) < iota((count, count), 1)
    place = jnp.sum(jnp.where((across == down) & earlier, 1.0, 0.0), axis=0, keepdims=True)
    swap = (lax.axis_index("cls") >> 1) & 1
    return (labels_row ^ swap) * SLOTS + place.astype(jnp.int32)


def row_of_slot(slots):
    return (slots & ~12) | ((slots & 4) << 1) | ((slots & 8) >> 1)


def alternate(first, second, own, group):
    rows, width = first.shape
    groups = (rows // group, group, width)
    first, second = first.reshape(groups), second.reshape(groups)
    even, odd = jnp.where(own, first, second), jnp.where(own, second, first)
    return jnp.concatenate([even[:, None], odd[:, None]], axis=1).reshape(2 * rows, width)


def pieces(sizes):
    starts = [sum(sizes[:i]) for i in range(len(sizes))]
    return [pl.ds(start, size) for start, size in zip(starts, sizes)]


def pack_kernel(sizes, labels_ref, rows_hbm, out_hbm, rows_ref, select_ref, out_ref, in_sems, out_sems):
    columns = pieces(sizes)
    width = out_ref.shape[1]
    loads = [
        [
            pltpu.make_async_copy(
                rows_hbm.at[:, pl.ds(part * width + at.start, at.size)],
                rows_ref.at[part, :, at],
                in_sems.at[part, j],
            )
            for part in range(PARTS)
        ]
        for j, at in enumerate(columns)
    ]
    stores = [
        pltpu.make_async_copy(out_ref.at[:, at], out_hbm.at[:, at], out_sems.at[j])
        for j, at in enumerate(columns)
    ]
    for pair in loads:
        for load in pair:
            load.start()
    each = TILE // PARTS
    row = row_of_slot(slot_of_row(labels_ref[...]))
    index = iota(select_ref.shape[1:], 0)
    for part in range(PARTS):
        chosen = index == row ^ (part * each)
        select_ref[part] = jnp.where(chosen, 1.0, 0.0).astype(BF16)
    own = iota((1, PACKED, 1), 1) & each == 0
    for j, at in enumerate(columns):
        for load in loads[j]:
            load.wait()
        parts = [
            jnp.dot(select_ref[part], rows_ref[part, :, at], preferred_element_type=F32)
            for part in range(PARTS)
        ]
        out_ref[:, at] = alternate(*parts, own, PACKED).astype(BF16)
        stores[j].start()
    for store in stores:
        store.wait()


def pack(labels_row, visibilities, rows, sizes):
    count, width = visibilities.shape[0], sum(sizes)
    anywhere = pl.BlockSpec(memory_space=pl.ANY)
    return pl.pallas_call(
        functools.partial(pack_kernel, sizes),
        in_specs=[pl.BlockSpec(memory_space=pltpu.VMEM), anywhere],
        out_specs=anywhere,
        out_shape=pltpu.HBM((rows, width), BF16),
        scratch_shapes=[
            pltpu.VMEM((PARTS, count, width), BF16),
            pltpu.VMEM((PARTS, rows // PARTS, count), BF16),
            pltpu.VMEM((rows, width), BF16),
            pltpu.SemaphoreType.DMA((PARTS, len(sizes))),
            pltpu.SemaphoreType.DMA((len(sizes),)),
        ],
        compiler_params=pltpu.CompilerParams(vmem_limit_bytes=24 << 20),
        name="pack",
    )(labels_row, visibilities)


def index_kernel(labels_ref, pairs_ref, source_ref, second_ref):
    count = labels_ref.shape[1]
    place = row_of_slot(slot_of_row(labels_ref[...]))
    local = (pairs_ref[...] & (count - 1)).astype(F32)
    first = jnp.broadcast_to(local[0:1], (count, count))
    other = jnp.broadcast_to(local[1:2], (count, count))
    first_down = first.T.astype(jnp.int32)
    lane = iota((count, count), 1)
    source = jnp.sum(
        jnp.where(first_down == lane, place.astype(F32), 0.0), axis=1, keepdims=True
    ).astype(jnp.int32)
    source_ref[...] = source
    second_ref[...] = jnp.where(other.T == first, 1.0, 0.0).astype(BF16)


def indices(labels_row, pairs_rows):
    count = labels_row.shape[1]
    return pl.pallas_call(
        index_kernel,
        out_shape=(
            jax.ShapeDtypeStruct((count, 1), jnp.int32),
            jax.ShapeDtypeStruct((count, count), BF16),
        ),
        compiler_params=pltpu.CompilerParams(vmem_limit_bytes=24 << 20),
        name="indices",
    )(labels_row, pairs_rows)


def as_column(row):
    lanes = 128
    parts = [
        jnp.broadcast_to(row[:, i : i + lanes], (lanes, lanes)).T[:, 0:1]
        for i in range(0, row.shape[1], lanes)
    ]
    return jnp.concatenate(parts, axis=0)


def table_kernel(coarse_cos_ref, coarse_sin_ref, fine_cos_ref, fine_sin_ref, taper_ref, out_ref):
    fine, half = fine_cos_ref.shape
    scale = 1.0 / math.sqrt(PARTS * half)
    fine_cos, fine_sin = fine_cos_ref[...], fine_sin_ref[...]
    start = iota((fine, half), 1) == 0
    turn = jnp.where(iota((fine, half), 0) & 1 == 0, scale, -scale)
    taper = as_column(taper_ref[...])
    for i in range(out_ref.shape[1] // fine):
        coarse_cos, coarse_sin = coarse_cos_ref[i : i + 1, :], coarse_sin_ref[i : i + 1, :]
        at = pl.ds(i * fine, fine)
        cosines = coarse_cos * fine_cos - coarse_sin * fine_sin
        sines = coarse_sin * fine_cos + coarse_cos * fine_sin
        sines = jnp.where(start, turn, sines)
        for table, columns in ((cosines, pl.ds(0, half)), (sines, pl.ds(half, half))):
            tapered = table.astype(BF16).astype(F32) * taper[i * fine : (i + 1) * fine]
            high = tapered.astype(BF16)
            out_ref[0, at, columns] = high
            out_ref[1, at, columns] = (tapered - high.astype(F32)).astype(BF16)


def tapered_tables(width, taper_row, fine):
    half = width // 2

    def angles(rows, spacing):
        n = jnp.arange(rows, dtype=jnp.int32) * spacing
        phase = n[:, None] * jnp.arange(half, dtype=jnp.int32)[None, :] % width
        return phase.astype(F32) * (2.0 * math.pi / width)

    coarse, small = angles(width // fine, fine), angles(fine, 1)
    scale = 1.0 / math.sqrt(width)
    return pl.pallas_call(
        table_kernel,
        out_shape=jax.ShapeDtypeStruct((2, width, width), BF16),
        compiler_params=pltpu.CompilerParams(vmem_limit_bytes=24 << 20),
        name="tables",
    )(jnp.cos(coarse) * scale, jnp.sin(coarse) * scale, jnp.cos(small), jnp.sin(small), taper_row)


def combine_kernel(filters_ref, flags_ref, table_ref, out_ref):
    flags = jnp.where(pl.program_id(0) == 0, flags_ref[0:1, :], flags_ref[1:2, :])
    keep = as_column((1 - flags).astype(F32))
    matrix = filters_ref[0]
    product = jnp.dot(matrix, table_ref[0], preferred_element_type=F32)
    product = product + jnp.dot(matrix, table_ref[1], preferred_element_type=F32)
    out_ref[0] = (product * keep).astype(BF16)


def combine(filters, flags, table, step):
    classes, width, _ = filters.shape
    block = pl.BlockSpec((1, step, width), lambda w, i: (w, i, 0))
    return pl.pallas_call(
        combine_kernel,
        grid=(classes, width // step),
        in_specs=[
            block,
            pl.BlockSpec((classes, step), lambda w, i: (0, i)),
            pl.BlockSpec((2, width, width), lambda w, i: (0, 0, 0), pipeline_mode=pl.Buffered(1)),
        ],
        out_specs=block,
        out_shape=pltpu.HBM((classes, width, width), BF16),
        compiler_params=pltpu.CompilerParams(vmem_limit_bytes=36 << 20),
        name="combine",
    )(filters, flags, table)


def filter_kernel(sizes, step, arrived_ref, matrix_hbm, out_hbm, split_ref, matrix_ref, out_ref, in_sems, out_sems):
    rows, width = arrived_ref.shape
    columns = pieces(sizes)
    loads = [
        pltpu.make_async_copy(matrix_hbm.at[:, :, at], matrix_ref.at[:, :, at], in_sems.at[j])
        for j, at in enumerate(columns)
    ]
    own = iota((1, PACKED, 1), 1) & SLOTS == 0
    loads[0].start()
    groups = len(loads) - 1
    count = rows // (2 * groups)
    for g in range(groups):
        arrived = arrived_ref[pl.ds(2 * g * count, 2 * count), :]
        arrived = arrived.reshape(count // PACKED, 2, PACKED, width)
        even, odd = arrived[:, 0], arrived[:, 1]
        first, second = jnp.where(own, even, odd), jnp.where(own, odd, even)
        split_ref[0, pl.ds(g * count, count), :] = first.reshape(count, width)
        split_ref[1, pl.ds(g * count, count), :] = second.reshape(count, width)
        loads[g + 1].start()
    stores = []
    for load, piece in zip(loads, columns):
        load.wait()
        for start in range(piece.start, piece.start + piece.size, step):
            at = pl.ds(start, step)
            done = [
                jnp.dot(split_ref[w], matrix_ref[w, :, at], preferred_element_type=F32)
                for w in range(2)
            ]
            out_ref[:, at] = alternate(*done, own, PACKED).astype(BF16)
            store = pltpu.make_async_copy(
                out_ref.at[:, at], out_hbm.at[:, at], out_sems.at[len(stores)]
            )
            store.start()
            stores.append(store)
    for store in stores:
        store.wait()


def filter_rows(arrived, matrices, sizes, step):
    rows, width = arrived.shape
    anywhere = pl.BlockSpec(memory_space=pl.ANY)
    return pl.pallas_call(
        functools.partial(filter_kernel, sizes, step),
        in_specs=[pl.BlockSpec(memory_space=pltpu.VMEM), anywhere],
        out_specs=anywhere,
        out_shape=pltpu.HBM((rows, width), BF16),
        scratch_shapes=[
            pltpu.VMEM((2, rows // 2, width), BF16),
            pltpu.VMEM((2, width, width), BF16),
            pltpu.VMEM((rows, width), BF16),
            pltpu.SemaphoreType.DMA((len(sizes),)),
            pltpu.SemaphoreType.DMA((width // step,)),
        ],
        compiler_params=pltpu.CompilerParams(vmem_limit_bytes=40 << 20),
        name="filter",
    )(arrived, matrices)


def power_kernel(returned_ref, source_ref, second_ref, out_hbm, out_ref, sems):
    count = second_ref.shape[0]
    rows, width = returned_ref.shape
    half, lanes, step = width // 2, 128, 256
    second = second_ref[...]
    each = TILE // PARTS
    index = iota((count, rows // PARTS), 1)
    fetch = [
        jnp.where(index == source_ref[...] ^ (part * each), 1.0, 0.0).astype(BF16)
        for part in range(PARTS)
    ]
    own = iota((1, PACKED, 1), 1) & each == 0

    def fetched(at):
        groups = returned_ref[:, at].reshape(rows // (2 * PACKED), 2, PACKED, step)
        even, odd = groups[:, 0], groups[:, 1]
        parts = [jnp.where(own, even, odd), jnp.where(own, odd, even)]
        return [
            jnp.dot(chosen, part.reshape(-1, step), preferred_element_type=F32)
            for chosen, part in zip(fetch, parts)
        ]

    mirror = (lanes - iota((count, lanes), 1)) & (lanes - 1)
    start = iota((count, step), 1) == 0
    edge = iota((count, lanes), 1) == 0
    blocks = half // lanes
    stores = []

    def store(at):
        copy = pltpu.make_async_copy(out_ref.at[:, at], out_hbm.at[:, at], sems.at[len(stores)])
        copy.start()
        stores.append(copy)

    def spectra(sums, j):
        cos_real, cos_imag, sin_real, sin_imag = sums
        far_real, far_imag = cos_real, cos_imag
        if j == 0:
            far_real = jnp.where(start, sin_real, cos_real)
            far_imag = jnp.where(start, sin_imag, cos_imag)
            sin_real = jnp.where(start, 0.0, sin_real)
            sin_imag = jnp.where(start, 0.0, sin_imag)
        return (
            (cos_real + sin_imag, cos_imag - sin_real),
            (far_real - sin_imag, far_imag + sin_real),
        )

    mirrored = []
    waiting = list(range(blocks))
    for j in range(half // step):
        at = pl.ds(j * step, step)
        far_at = pl.ds(half + j * step, step)
        sums = fetched(at) + fetched(far_at)
        others = jnp.dot(
            second, jnp.concatenate(sums, axis=1).astype(BF16), preferred_element_type=F32
        )
        others = [others[:, i * step : (i + 1) * step] for i in range(2 * PARTS)]
        near, far = [
            one[0] * two[0] + one[1] * two[1]
            for one, two in zip(spectra(sums, j), spectra(others, j))
        ]
        out_ref[:, at] = near
        store(at)
        for block in range(step // lanes):
            part = far[:, block * lanes : (block + 1) * lanes]
            mirrored.append(jnp.take_along_axis(part, mirror, axis=1))
        for b in list(waiting):
            edge_from, rest_from = (blocks - b) % blocks, blocks - 1 - b
            if max(edge_from, rest_from) < len(mirrored):
                waiting.remove(b)
                there = pl.ds(half + b * lanes, lanes)
                out_ref[:, there] = jnp.where(edge, mirrored[edge_from], mirrored[rest_from])
                store(there)
    for copy in stores:
        copy.wait()


def cross_power(returned, source, second):
    width = returned.shape[1]
    count = second.shape[0]
    in_vmem = pl.BlockSpec(memory_space=pltpu.VMEM)
    return pl.pallas_call(
        power_kernel,
        in_specs=[in_vmem, in_vmem, in_vmem],
        out_specs=pl.BlockSpec(memory_space=pl.ANY),
        out_shape=pltpu.HBM((count, width), F32),
        scratch_shapes=[
            pltpu.VMEM((count, width), F32),
            pltpu.SemaphoreType.DMA((width // 256 // 2 + width // 128 // 2,)),
        ],
        compiler_params=pltpu.CompilerParams(vmem_limit_bytes=24 << 20),
        name="power",
    )(returned, source, second)


def exchange(packed, peers):
    rows, width = packed.shape
    moved = lax.all_to_all(
        packed.reshape(peers, rows // peers, width),
        ("tm", "cls"),
        split_axis=0,
        concat_axis=0,
        tiled=True,
    )
    return moved.reshape(rows, width)


def local(visibilities, row_class, filters, flags, taper, pairs):
    count = visibilities.shape[0]
    classes, width = filters.shape[0], filters.shape[1]
    peers = lax.axis_size(("tm", "cls"))
    rows = peers * TILE
    assert classes == 2 and count & (count - 1) == 0
    labels_row = row_class.reshape(1, count)
    in_hbm = lambda x: pltpu.with_memory_space_constraint(x, pltpu.HBM)
    packed = pack(in_hbm(labels_row), in_hbm(visibilities), rows, split_width(width, (1, 1, 1)))
    arrived = exchange(packed, peers)
    source, second = indices(labels_row, pairs.T)
    table = tapered_tables(width, taper.reshape(1, width), 32)
    matrices = combine(in_hbm(filters), flags, table, 512)
    summed = filter_rows(arrived, in_hbm(matrices), split_width(width, (1, 2, 3)), 256)
    returned = exchange(summed, peers)
    return cross_power(returned, source, second)


def solution(mesh):
    across = ("tm", "cls")
    placed = (
        P(across, None),
        P(across, None),
        P(across, None, None),
        P(across, None),
        P(),
        P(across, None),
    )
    return jax.shard_map(
        local, mesh=mesh, in_specs=placed, out_specs=P(across, None), check_vma=False
    )
```
